32 devices in a mesh: outer: 4 (over y, core), inner: 8 (over z, x).
Axes of the slice: x: 2, y: 2, z: 4, core: 2. Of those that a mesh axis runs over, the one named last changes fastest.
Arguments:
- matrix_panel: float32 [32, 65536], P(None, ('outer', 'inner')), may hold values from -6 to 6
- row_signs: int32 [65536], P(('outer', 'inner')), may hold values from -1 to 1, as said below
- kept_rows: int32 [4096], replicated, may hold values from 0 to 65535, as said below
Outputs:
- sketch: float32 [4096, 32], P(('outer', 'inner'))
The draws below stay inside these ranges and needn't reach their ends.
Inputs may be any that keep to these rules, and one draw needn't show every extreme that they name: `row_signs`: each entry is -1 or 1. `kept_rows`: distinct row numbers.
All inputs are finite; a program needn't handle non-finite values.
Results may differ from the reference program's by a relative error of at most 0.00007.
Values sent between devices are 32-bit elements; how exact they have to be, the bound alone decides.
A program may use at most 64 MiB of HBM per device.

```python
import math
import jax
import jax.numpy as jnp
from jax import lax

COLS = 32
ROWS = 65536
KEPT = 4096


def draw_row_signs(key, part):
    return (2 * jax.random.randint(key, (ROWS,), 0, 2) - 1).astype(jnp.int32)


def draw_kept_rows(key, part):
    inside = jax.random.choice(jax.random.fold_in(key, 11), ROWS - 2, (KEPT - 2,), replace=False).astype(jnp.int32) + 1
    ends = jnp.array([0, ROWS - 1], dtype=jnp.int32)
    joined = jnp.concatenate([ends, inside])
    return jax.random.permutation(jax.random.fold_in(key, 23), joined).astype(jnp.int32)


def block_scale(rng, dims, split, low, top_value):
    loudness = 1.0
    for dim, shards_of in split:
        draws = jax.random.uniform(jax.random.fold_in(jax.random.fold_in(rng, 6), dim), (shards_of,), jnp.float32, low / len(split), top_value / len(split))
        loudness = loudness * jnp.repeat(jnp.exp(draws), dims[dim] // shards_of).reshape((-1,) + (1,) * (len(dims) - 1 - dim))
    return loudness


def noise(rng, dims, scale, bound, split=(), kind=jnp.bfloat16):
    loudness = block_scale(rng, dims, split, -0.22, 0.18) if split else 1.0
    result = jax.random.normal(rng, dims, jnp.float32) * scale * loudness
    return jnp.minimum(jnp.maximum(result, -bound), bound).astype(kind)


def setup_inputs(seed: int = 0) -> dict:
    key_of = jax.random.split(jax.random.key(seed), 4)
    return {
        "matrix_panel": noise(key_of[0], (COLS, ROWS), 1.0, 6.0, ((1, 32),), jnp.float32),
        "row_signs": draw_row_signs(jax.random.fold_in(key_of[3], 71), 0),
        "kept_rows": draw_kept_rows(jax.random.fold_in(key_of[3], 71), 0),
    }


def walsh_transform(vector):
    bit_total = ROWS.bit_length() - 1
    stride = 1
    done_bits = 0
    while done_bits < bit_total:
        if bit_total - done_bits >= 2:
            shaped = vector.reshape(-1, 4, stride)
            first = shaped[:, 0] + shaped[:, 1]
            second = shaped[:, 0] - shaped[:, 1]
            third = shaped[:, 2] + shaped[:, 3]
            fourth = shaped[:, 2] - shaped[:, 3]
            shaped = jnp.stack([first + third, second + fourth, first - third, second - fourth], axis=1)
            stride = stride * 4
            done_bits = done_bits + 2
        else:
            shaped = vector.reshape(-1, 2, stride)
            shaped = jnp.stack([shaped[:, 0] + shaped[:, 1], shaped[:, 0] - shaped[:, 1]], axis=1)
            stride = stride * 2
            done_bits = done_bits + 1
        vector = shaped.reshape(-1)
    return vector

def reference(matrix_panel, row_signs, kept_rows):
    signed = matrix_panel * row_signs.astype(jnp.float32)[None, :]

    def sketch_column(column):
        return walsh_transform(column)[kept_rows]
    picked = lax.map(sketch_column, signed)
    return picked.T * (1.0 / math.sqrt(ROWS))
```

```python
import functools
import math

import jax
import jax.numpy as jnp
from jax import lax
from jax.experimental import pallas as pl
from jax.experimental.pallas import tpu as pltpu
from jax.sharding import PartitionSpec as P

MESH = pl.DeviceIdType.MESH
LANES = 128
SHARE = 4


def bit_parity(values):
    folded = jnp.bitwise_xor(values, jnp.right_shift(values, 16))
    folded = jnp.bitwise_xor(folded, jnp.right_shift(folded, 8))
    folded = jnp.bitwise_xor(folded, jnp.right_shift(folded, 4))
    folded = jnp.bitwise_xor(folded, jnp.right_shift(folded, 2))
    folded = jnp.bitwise_xor(folded, jnp.right_shift(folded, 1))
    return jnp.bitwise_and(folded, 1)


def hadamard(order_size):
    positions = lax.iota(jnp.int32, order_size)
    shared = jnp.bitwise_and(positions[:, None], positions[None, :])
    return jnp.where(bit_parity(shared) == 0, 1.0, -1.0).astype(jnp.float32)


def scatter_form(matrix_panel, row_signs, kept_rows):
    highest = lax.Precision.HIGHEST
    columns, local_rows = matrix_panel.shape
    outer_count = lax.axis_size("outer")
    inner_count = lax.axis_size("inner")
    device_count = outer_count * inner_count
    total_rows = local_rows * device_count
    me_outer = lax.axis_index("outer")
    me_inner = lax.axis_index("inner")
    signed = matrix_panel * row_signs.astype(jnp.float32)[None, :]
    leading = 128
    trailing = local_rows // leading
    blocks = signed.reshape(columns, leading, trailing)
    blocks = jnp.einsum("ap,jpq->jaq", hadamard(leading), blocks, precision=highest)
    blocks = jnp.einsum("bq,jaq->jab", hadamard(trailing), blocks, precision=highest)
    local_mix = blocks.reshape(columns, local_rows)
    low_bits = kept_rows % local_rows
    high_outer = kept_rows // (local_rows * inner_count)
    high_inner = kept_rows // local_rows % inner_count
    flips = bit_parity(jnp.bitwise_and(high_outer, me_outer)) + bit_parity(
        jnp.bitwise_and(high_inner, me_inner)
    )
    parity_sign = jnp.where(flips % 2 == 0, 1.0, -1.0).astype(jnp.float32)
    values = jnp.take(local_mix, low_bits, axis=1)
    summed = lax.psum_scatter(
        (values * parity_sign[None, :]).T, ("outer", "inner"), scatter_dimension=0, tiled=True
    )
    return summed * (1.0 / math.sqrt(total_rows))


def flipped(index, mask, size):
    result, bit = 0, 1
    while bit < size:
        digit = index // bit % 2
        result = result + (1 - digit if mask & bit else digit) * bit
        bit *= 2
    return result


def log2(size):
    return size.bit_length() - 1


def sign_of_bit(rows, bit):
    return (1 - 2 * jnp.bitwise_and(jnp.right_shift(rows, bit), 1)).astype(jnp.float32)


def kernel(
    outer_count, inner_count, low_count, scale,
    panel_ref, signs_ref, kept_ref, out_ref,
    send1, recv1, send2, recv2, mix_ref, bits_ref, final_ref,
    send1_sem, recv1_sem, send2_sem, recv2_sem,
):
    device_count = outer_count * inner_count
    high_count = inner_count // low_count
    group = outer_count * low_count
    columns, local_rows = panel_ref.shape
    kept_count = kept_ref.shape[1]
    mids = local_rows // LANES
    rows = mids * SHARE
    me_outer = lax.axis_index("outer")
    me_inner = lax.axis_index("inner")
    me = me_outer * inner_count + me_inner
    me_high = me_inner // low_count
    me_low = me_inner % low_count
    me_group = me_outer * low_count + me_low

    barrier = pltpu.get_barrier_semaphore()

    def greet(step, carry):
        other = (me + step) % device_count
        pl.semaphore_signal(
            barrier, inc=1, device_id=(other // inner_count, other % inner_count), device_id_type=MESH
        )
        return carry

    lax.fori_loop(1, device_count, greet, 0)

    for mid in range(mids):
        lanes = slice(mid * LANES, (mid + 1) * LANES)
        block = panel_ref[:, lanes] * signs_ref[:, lanes].astype(jnp.float32)
        for peer in range(group):
            send1[peer, mid * SHARE:(mid + 1) * SHARE, :] = block[peer * SHARE:(peer + 1) * SHARE, :]

    pl.semaphore_wait(barrier, device_count - 1)

    copies = []
    for mask in sorted(range(1, group), key=lambda m: (-bin(m).count("1"), -m)):
        peer = flipped(me_group, mask, group)
        copy = pltpu.make_async_remote_copy(
            src_ref=send1.at[peer],
            dst_ref=recv1.at[me_group],
            send_sem=send1_sem.at[mask],
            recv_sem=recv1_sem.at[mask],
            device_id=(peer // low_count, me_high * low_count + peer % low_count),
            device_id_type=MESH,
        )
        copy.start()
        copies.append(copy)
    recv1[me_group] = send1[me_group]

    span = 4 * LANES
    low_bits = log2(LANES)
    inner_bits = log2(inner_count)
    fold_bits = [log2(local_rows) + inner_bits + b for b in reversed(range(log2(outer_count)))]
    fold_bits += [log2(local_rows) + b for b in reversed(range(log2(low_count)))]
    fold_bits += [b for b in reversed(range(low_bits, log2(local_rows)))]

    def signs_of(chunk, carry):
        lanes = pl.ds(pl.multiple_of(chunk * span, span), span)
        kept = kept_ref[:, lanes]
        for place, bit in enumerate(fold_bits):
            bits_ref[place:place + 1, lanes] = sign_of_bit(kept, bit)
        position = lax.broadcasted_iota(jnp.int32, (16, span), 0)
        base = jnp.ones((16, span), jnp.float32)
        for bit in range(4):
            taken = jnp.bitwise_and(jnp.right_shift(position, bit), 1) == 1
            base = base * jnp.where(taken, sign_of_bit(kept, bit), 1.0)
        for top in range(LANES // 16):
            block = base
            for bit in range(4, low_bits):
                if top >> (bit - 4) & 1:
                    block = block * sign_of_bit(kept, bit)
            block = block.astype(jnp.bfloat16)
            mix_ref[top * 16:(top + 1) * 16, lanes] = block
            mix_ref[LANES + top * 16:LANES + (top + 1) * 16, lanes] = block
        return carry

    lax.fori_loop(0, kept_count // span, signs_of, 0)

    for copy in copies:
        copy.wait_recv()

    gathered = recv1[...].reshape(group * rows, LANES)
    upper = gathered.astype(jnp.bfloat16)
    lower = (gathered - upper.astype(jnp.float32)).astype(jnp.bfloat16)
    both = jnp.concatenate([upper, lower], axis=1)

    mine = me_high * group + me_group
    width = low_count * LANES
    far = [(h, o) for h in reversed(range(high_count)) for o in reversed(range(outer_count))]
    sent = []
    for high_mask, outer_mask in far:
        high = flipped(me_high, high_mask, high_count)
        outer = flipped(me_outer, outer_mask, outer_count)
        block = outer * high_count + high
        lanes = pl.ds(pl.multiple_of(block * width, width), width)
        part = jnp.dot(both, mix_ref[:, lanes], preferred_element_type=jnp.float32)
        for place in range(len(fold_bits)):
            half = part.shape[0] // 2
            part = part[:half] + part[half:] * bits_ref[place:place + 1, lanes]
        for low in range(low_count):
            to = block * low_count + low
            piece = part[:, low * LANES:(low + 1) * LANES]
            send2[to] = piece
            copy = pltpu.make_async_remote_copy(
                src_ref=send2.at[to],
                dst_ref=recv2.at[mine],
                send_sem=send2_sem.at[to],
                recv_sem=recv2_sem.at[mine],
                device_id=(outer, high * low_count + low),
                device_id_type=MESH,
            )
            if high_mask == 0 and outer_mask == 0:
                @pl.when(low == me_low)
                def _():
                    recv2[mine] = piece

                @pl.when(low != me_low)
                def _():
                    copy.start()
            else:
                copy.start()

    kept = kept_ref[:, pl.ds(pl.multiple_of(me * LANES, LANES), LANES)]
    high_signs = [sign_of_bit(kept, log2(local_rows * low_count) + b) for b in range(log2(high_count))]

    def arrival(source):
        return pltpu.make_async_remote_copy(
            src_ref=send2.at[source],
            dst_ref=recv2.at[source],
            send_sem=send2_sem.at[source],
            recv_sem=recv2_sem.at[source],
            device_id=(me_outer, me_inner),
            device_id_type=MESH,
        )

    def await_arrival(step, carry):
        arrival((mine + step) % device_count).wait_recv()
        return carry

    lax.fori_loop(1, device_count, await_arrival, 0)

    for peer in range(group):
        total = recv2[peer]
        for high in range(1, high_count):
            term = recv2[high * group + peer]
            for bit, sign in enumerate(high_signs):
                if high >> bit & 1:
                    term = term * sign
            total = total + term
        final_ref[peer * SHARE:(peer + 1) * SHARE, :] = total * scale
    out_ref[...] = final_ref[...].T

    def await_sent(step, carry):
        arrival((me + step) % device_count).wait_send()
        return carry

    lax.fori_loop(1, device_count, await_sent, 0)
    for copy in copies:
        copy.wait_send()


def solution(mesh):
    outer_count, inner_count = mesh.shape["outer"], mesh.shape["inner"]
    device_count = outer_count * inner_count

    def local(matrix_panel, row_signs, kept_rows):
        columns, local_rows = matrix_panel.shape
        kept_count = kept_rows.shape[0]
        low_count = max(columns // (SHARE * outer_count), 1)
        fits = (
            low_count * outer_count * SHARE == columns
            and inner_count % low_count == 0
            and kept_count == device_count * LANES
            and local_rows % (2 * LANES) == 0
        )
        if not fits:
            return scatter_form(matrix_panel, row_signs, kept_rows)
        group = outer_count * low_count
        rows = local_rows // LANES * SHARE
        bits = log2(group) + log2(local_rows // LANES)
        in_vmem = pl.BlockSpec(memory_space=pltpu.VMEM)
        return pl.pallas_call(
            functools.partial(
                kernel, outer_count, inner_count, low_count, 1.0 / math.sqrt(local_rows * device_count)
            ),
            out_shape=jax.ShapeDtypeStruct((LANES, columns), jnp.float32),
            in_specs=[in_vmem] * 3,
            out_specs=in_vmem,
            scratch_shapes=[
                pltpu.VMEM((group, rows, LANES), jnp.float32),
                pltpu.VMEM((group, rows, LANES), jnp.float32),
                pltpu.VMEM((device_count, SHARE, LANES), jnp.float32),
                pltpu.VMEM((device_count, SHARE, LANES), jnp.float32),
                pltpu.VMEM((2 * LANES, kept_count), jnp.bfloat16),
                pltpu.VMEM((bits, kept_count), jnp.float32),
                pltpu.VMEM((columns, LANES), jnp.float32),
                pltpu.SemaphoreType.DMA((group,)),
                pltpu.SemaphoreType.DMA((group,)),
                pltpu.SemaphoreType.DMA((device_count,)),
                pltpu.SemaphoreType.DMA((device_count,)),
            ],
            compiler_params=pltpu.CompilerParams(collective_id=0, has_side_effects=True),
        )(matrix_panel, row_signs.reshape(1, local_rows), kept_rows.reshape(1, kept_count))

    return jax.shard_map(
        local,
        mesh=mesh,
        in_specs=(P(None, ("outer", "inner")), P(("outer", "inner")), P()),
        out_specs=P(("outer", "inner"), None),
        check_vma=False,
    )
```

```python
import functools
import math

import jax
import jax.numpy as jnp
from jax import lax
from jax.experimental import pallas as pl
from jax.experimental.pallas import tpu as pltpu
from jax.sharding import PartitionSpec as P

MESH = pl.DeviceIdType.MESH
LANES = 128
SHARE = 4


def bit_parity(values):
    folded = jnp.bitwise_xor(values, jnp.right_shift(values, 16))
    folded = jnp.bitwise_xor(folded, jnp.right_shift(folded, 8))
    folded = jnp.bitwise_xor(folded, jnp.right_shift(folded, 4))
    folded = jnp.bitwise_xor(folded, jnp.right_shift(folded, 2))
    folded = jnp.bitwise_xor(folded, jnp.right_shift(folded, 1))
    return jnp.bitwise_and(folded, 1)


def hadamard(order_size):
    positions = lax.iota(jnp.int32, order_size)
    shared = jnp.bitwise_and(positions[:, None], positions[None, :])
    return jnp.where(bit_parity(shared) == 0, 1.0, -1.0).astype(jnp.float32)


def scatter_form(matrix_panel, row_signs, kept_rows):
    highest = lax.Precision.HIGHEST
    columns, local_rows = matrix_panel.shape
    outer_count = lax.axis_size("outer")
    inner_count = lax.axis_size("inner")
    device_count = outer_count * inner_count
    total_rows = local_rows * device_count
    me_outer = lax.axis_index("outer")
    me_inner = lax.axis_index("inner")
    signed = matrix_panel * row_signs.astype(jnp.float32)[None, :]
    leading = 128
    trailing = local_rows // leading
    blocks = signed.reshape(columns, leading, trailing)
    blocks = jnp.einsum("ap,jpq->jaq", hadamard(leading), blocks, precision=highest)
    blocks = jnp.einsum("bq,jaq->jab", hadamard(trailing), blocks, precision=highest)
    local_mix = blocks.reshape(columns, local_rows)
    low_bits = kept_rows % local_rows
    high_outer = kept_rows // (local_rows * inner_count)
    high_inner = kept_rows // local_rows % inner_count
    flips = bit_parity(jnp.bitwise_and(high_outer, me_outer)) + bit_parity(
        jnp.bitwise_and(high_inner, me_inner)
    )
    parity_sign = jnp.where(flips % 2 == 0, 1.0, -1.0).astype(jnp.float32)
    values = jnp.take(local_mix, low_bits, axis=1)
    summed = lax.psum_scatter(
        (values * parity_sign[None, :]).T, ("outer", "inner"), scatter_dimension=0, tiled=True
    )
    return summed * (1.0 / math.sqrt(total_rows))


def flipped(index, mask, size):
    result, bit = 0, 1
    while bit < size:
        digit = index // bit % 2
        result = result + (1 - digit if mask & bit else digit) * bit
        bit *= 2
    return result


def log2(size):
    return size.bit_length() - 1


def sign_of_bit(rows, bit):
    return (1 - 2 * jnp.bitwise_and(jnp.right_shift(rows, bit), 1)).astype(jnp.float32)


def kernel(
    outer_count, inner_count, low_count, scale,
    panel_hbm, signs_hbm, kept_hbm, out_ref,
    panel_ref, signs_ref, kept_ref, load_sem, ready_sem,
    send1, recv1, send2, recv2, mix_ref, bits_ref, final_ref,
    send1_sem, recv1_sem, send2_sem, recv2_sem,
):
    device_count = outer_count * inner_count
    high_count = inner_count // low_count
    group = outer_count * low_count
    columns, local_rows = panel_hbm.shape
    kept_count = kept_hbm.shape[1]
    mids = local_rows // LANES
    rows = mids * SHARE
    me_outer = lax.axis_index("outer")
    me_inner = lax.axis_index("inner")
    me = me_outer * inner_count + me_inner
    me_high = me_inner // low_count
    me_low = me_inner % low_count
    me_group = me_outer * low_count + me_low

    barrier = pltpu.get_barrier_semaphore()

    loads = [
        pltpu.make_async_copy(source, target, load_sem.at[place])
        for place, (source, target) in enumerate(
            [(panel_hbm, panel_ref), (signs_hbm, signs_ref), (kept_hbm, kept_ref)]
        )
    ]
    for load in loads:
        load.start()

    def tell_group(semaphore):
        for step in range(1, group):
            peer = (me_group + step) % group
            pl.semaphore_signal(
                semaphore,
                inc=1,
                device_id=(peer // low_count, me_high * low_count + peer % low_count),
                device_id_type=MESH,
            )

    for step in range(1, high_count):
        high = (me_high + step) % high_count
        pl.semaphore_signal(
            barrier, inc=1, device_id=(me_outer, high * low_count + me_low), device_id_type=MESH
        )
    tell_group(barrier)
    for load in loads:
        load.wait()

    for mid in range(mids):
        lanes = slice(mid * LANES, (mid + 1) * LANES)
        block = panel_ref[:, lanes] * signs_ref[:, lanes].astype(jnp.float32)
        for peer in range(group):
            send1[peer, mid * SHARE:(mid + 1) * SHARE, :] = block[peer * SHARE:(peer + 1) * SHARE, :]

    pl.semaphore_wait(barrier, group - 1 + high_count - 1)

    copies = []
    for mask in sorted(range(1, group), key=lambda m: (-bin(m).count("1"), -m)):
        peer = flipped(me_group, mask, group)
        copy = pltpu.make_async_remote_copy(
            src_ref=send1.at[peer],
            dst_ref=recv1.at[me_group],
            send_sem=send1_sem.at[mask],
            recv_sem=recv1_sem.at[mask],
            device_id=(peer // low_count, me_high * low_count + peer % low_count),
            device_id_type=MESH,
        )
        copy.start()
        copies.append(copy)
    tell_group(ready_sem)
    recv1[me_group] = send1[me_group]

    span = 4 * LANES
    low_bits = log2(LANES)
    inner_bits = log2(inner_count)
    fold_bits = [log2(local_rows) + inner_bits + b for b in reversed(range(log2(outer_count)))]
    fold_bits += [log2(local_rows) + b for b in reversed(range(log2(low_count)))]
    fold_bits += [b for b in reversed(range(low_bits, log2(local_rows)))]

    def signs_of(chunk, carry):
        lanes = pl.ds(pl.multiple_of(chunk * span, span), span)
        kept = kept_ref[:, lanes]
        for place, bit in enumerate(fold_bits):
            bits_ref[place:place + 1, lanes] = sign_of_bit(kept, bit)
        position = lax.broadcasted_iota(jnp.int32, (16, span), 0)
        base = jnp.ones((16, span), jnp.float32)
        for bit in range(4):
            taken = jnp.bitwise_and(jnp.right_shift(position, bit), 1) == 1
            base = base * jnp.where(taken, sign_of_bit(kept, bit), 1.0)
        for top in range(LANES // 16):
            block = base
            for bit in range(4, low_bits):
                if top >> (bit - 4) & 1:
                    block = block * sign_of_bit(kept, bit)
            block = block.astype(jnp.bfloat16)
            mix_ref[top * 16:(top + 1) * 16, lanes] = block
            mix_ref[LANES + top * 16:LANES + (top + 1) * 16, lanes] = block
        return carry

    lax.fori_loop(0, kept_count // span, signs_of, 0)

    for copy in copies:
        copy.wait_recv()

    gathered = recv1[...].reshape(group * rows, LANES)
    upper = gathered.astype(jnp.bfloat16)
    lower = (gathered - upper.astype(jnp.float32)).astype(jnp.bfloat16)
    both = jnp.concatenate([upper, lower], axis=1)

    pl.semaphore_wait(ready_sem, group - 1)
    mine = me_high * group + me_group
    width = low_count * LANES
    far = [(h, o) for h in reversed(range(high_count)) for o in reversed(range(outer_count))]
    sent = []
    for high_mask, outer_mask in far:
        high = flipped(me_high, high_mask, high_count)
        outer = flipped(me_outer, outer_mask, outer_count)
        block = outer * high_count + high
        lanes = pl.ds(pl.multiple_of(block * width, width), width)
        part = jnp.dot(both, mix_ref[:, lanes], preferred_element_type=jnp.float32)
        for place in range(len(fold_bits)):
            half = part.shape[0] // 2
            part = part[:half] + part[half:] * bits_ref[place:place + 1, lanes]
        for low in range(low_count):
            to = block * low_count + low
            piece = part[:, low * LANES:(low + 1) * LANES]
            send2[to] = piece
            copy = pltpu.make_async_remote_copy(
                src_ref=send2.at[to],
                dst_ref=recv2.at[mine],
                send_sem=send2_sem.at[to],
                recv_sem=recv2_sem.at[mine],
                device_id=(outer, high * low_count + low),
                device_id_type=MESH,
            )
            if high_mask == 0 and outer_mask == 0:
                @pl.when(low == me_low)
                def _():
                    recv2[mine] = piece

                @pl.when(low != me_low)
                def _():
                    copy.start()
            else:
                copy.start()

    kept = kept_ref[:, pl.ds(pl.multiple_of(me * LANES, LANES), LANES)]
    high_signs = [sign_of_bit(kept, log2(local_rows * low_count) + b) for b in range(log2(high_count))]

    def arrival(source):
        return pltpu.make_async_remote_copy(
            src_ref=send2.at[source],
            dst_ref=recv2.at[source],
            send_sem=send2_sem.at[source],
            recv_sem=recv2_sem.at[source],
            device_id=(me_outer, me_inner),
            device_id_type=MESH,
        )

    def await_arrival(step, carry):
        arrival((mine + step) % device_count).wait_recv()
        return carry

    lax.fori_loop(1, device_count, await_arrival, 0)

    for peer in range(group):
        total = recv2[peer]
        for high in range(1, high_count):
            term = recv2[high * group + peer]
            for bit, sign in enumerate(high_signs):
                if high >> bit & 1:
                    term = term * sign
            total = total + term
        final_ref[peer * SHARE:(peer + 1) * SHARE, :] = total * scale
    out_ref[...] = final_ref[...]

    def await_sent(step, carry):
        arrival((me + step) % device_count).wait_send()
        return carry

    lax.fori_loop(1, device_count, await_sent, 0)
    for copy in copies:
        copy.wait_send()


def solution(mesh):
    outer_count, inner_count = mesh.shape["outer"], mesh.shape["inner"]
    device_count = outer_count * inner_count

    def local(matrix_panel, row_signs, kept_rows):
        columns, local_rows = matrix_panel.shape
        kept_count = kept_rows.shape[0]
        low_count = max(columns // (SHARE * outer_count), 1)
        fits = (
            low_count * outer_count * SHARE == columns
            and inner_count % low_count == 0
            and kept_count == device_count * LANES
            and local_rows % (2 * LANES) == 0
        )
        if not fits:
            return scatter_form(matrix_panel, row_signs, kept_rows)
        group = outer_count * low_count
        rows = local_rows // LANES * SHARE
        bits = log2(group) + log2(local_rows // LANES)
        in_vmem = pl.BlockSpec(memory_space=pltpu.VMEM)
        return pl.pallas_call(
            functools.partial(
                kernel, outer_count, inner_count, low_count, 1.0 / math.sqrt(local_rows * device_count)
            ),
            out_shape=jax.ShapeDtypeStruct((columns, LANES), jnp.float32),
            in_specs=[pl.BlockSpec(memory_space=pl.ANY)] * 3,
            out_specs=in_vmem,
            scratch_shapes=[
                pltpu.VMEM((columns, local_rows), jnp.float32),
                pltpu.VMEM((1, local_rows), jnp.int32),
                pltpu.VMEM((1, kept_count), jnp.int32),
                pltpu.SemaphoreType.DMA((3,)),
                pltpu.SemaphoreType.REGULAR,
                pltpu.VMEM((group, rows, LANES), jnp.float32),
                pltpu.VMEM((group, rows, LANES), jnp.float32),
                pltpu.VMEM((device_count, SHARE, LANES), jnp.float32),
                pltpu.VMEM((device_count, SHARE, LANES), jnp.float32),
                pltpu.VMEM((2 * LANES, kept_count), jnp.bfloat16),
                pltpu.VMEM((bits, kept_count), jnp.float32),
                pltpu.VMEM((columns, LANES), jnp.float32),
                pltpu.SemaphoreType.DMA((group,)),
                pltpu.SemaphoreType.DMA((group,)),
                pltpu.SemaphoreType.DMA((device_count,)),
                pltpu.SemaphoreType.DMA((device_count,)),
            ],
            compiler_params=pltpu.CompilerParams(collective_id=0, has_side_effects=True),
        )(matrix_panel, row_signs.reshape(1, local_rows), kept_rows.reshape(1, kept_count)).T

    return jax.shard_map(
        local,
        mesh=mesh,
        in_specs=(P(None, ("outer", "inner")), P(("outer", "inner")), P()),
        out_specs=P(("outer", "inner"), None),
        check_vma=False,
    )
```

```python
import functools
import math

import jax
import jax.numpy as jnp
from jax import lax
from jax.experimental import pallas as pl
from jax.experimental.pallas import tpu as pltpu
from jax.sharding import PartitionSpec as P

MESH = pl.DeviceIdType.MESH
LANES = 128
SHARE = 4


def bit_parity(values):
    folded = jnp.bitwise_xor(values, jnp.right_shift(values, 16))
    folded = jnp.bitwise_xor(folded, jnp.right_shift(folded, 8))
    folded = jnp.bitwise_xor(folded, jnp.right_shift(folded, 4))
    folded = jnp.bitwise_xor(folded, jnp.right_shift(folded, 2))
    folded = jnp.bitwise_xor(folded, jnp.right_shift(folded, 1))
    return jnp.bitwise_and(folded, 1)


def hadamard(order_size):
    positions = lax.iota(jnp.int32, order_size)
    shared = jnp.bitwise_and(positions[:, None], positions[None, :])
    return jnp.where(bit_parity(shared) == 0, 1.0, -1.0).astype(jnp.float32)


def scatter_form(matrix_panel, row_signs, kept_rows):
    highest = lax.Precision.HIGHEST
    columns, local_rows = matrix_panel.shape
    outer_count = lax.axis_size("outer")
    inner_count = lax.axis_size("inner")
    device_count = outer_count * inner_count
    total_rows = local_rows * device_count
    me_outer = lax.axis_index("outer")
    me_inner = lax.axis_index("inner")
    signed = matrix_panel * row_signs.astype(jnp.float32)[None, :]
    leading = 128
    trailing = local_rows // leading
    blocks = signed.reshape(columns, leading, trailing)
    blocks = jnp.einsum("ap,jpq->jaq", hadamard(leading), blocks, precision=highest)
    blocks = jnp.einsum("bq,jaq->jab", hadamard(trailing), blocks, precision=highest)
    local_mix = blocks.reshape(columns, local_rows)
    low_bits = kept_rows % local_rows
    high_outer = kept_rows // (local_rows * inner_count)
    high_inner = kept_rows // local_rows % inner_count
    flips = bit_parity(jnp.bitwise_and(high_outer, me_outer)) + bit_parity(
        jnp.bitwise_and(high_inner, me_inner)
    )
    parity_sign = jnp.where(flips % 2 == 0, 1.0, -1.0).astype(jnp.float32)
    values = jnp.take(local_mix, low_bits, axis=1)
    summed = lax.psum_scatter(
        (values * parity_sign[None, :]).T, ("outer", "inner"), scatter_dimension=0, tiled=True
    )
    return summed * (1.0 / math.sqrt(total_rows))


def flipped(index, mask, size):
    result, bit = 0, 1
    while bit < size:
        digit = index // bit % 2
        result = result + (1 - digit if mask & bit else digit) * bit
        bit *= 2
    return result


def log2(size):
    return size.bit_length() - 1


def sign_of_bit(rows, bit):
    return (1 - 2 * jnp.bitwise_and(jnp.right_shift(rows, bit), 1)).astype(jnp.float32)


def kernel(
    outer_count, inner_count, low_count, scale,
    panel_hbm, signs_hbm, kept_hbm, recv2,
    panel_ref, signs_ref, kept_ref, load_sem, ready_sem,
    send1, recv1, send2, mix_ref, bits_ref,
    send1_sem, recv1_sem, send2_sem, recv2_sem, own_sem,
):
    device_count = outer_count * inner_count
    high_count = inner_count // low_count
    group = outer_count * low_count
    columns, local_rows = panel_hbm.shape
    kept_count = kept_hbm.shape[1]
    mids = local_rows // LANES
    rows = mids * SHARE
    me_outer = lax.axis_index("outer")
    me_inner = lax.axis_index("inner")
    me = me_outer * inner_count + me_inner
    me_high = me_inner // low_count
    me_low = me_inner % low_count
    me_group = me_outer * low_count + me_low

    barrier = pltpu.get_barrier_semaphore()

    loads = [
        pltpu.make_async_copy(source, target, load_sem.at[place])
        for place, (source, target) in enumerate(
            [(panel_hbm, panel_ref), (signs_hbm, signs_ref), (kept_hbm, kept_ref)]
        )
    ]
    for load in loads:
        load.start()

    def tell_group(semaphore):
        for step in range(1, group):
            peer = (me_group + step) % group
            pl.semaphore_signal(
                semaphore,
                inc=1,
                device_id=(peer // low_count, me_high * low_count + peer % low_count),
                device_id_type=MESH,
            )

    for step in range(1, high_count):
        high = (me_high + step) % high_count
        pl.semaphore_signal(
            barrier, inc=1, device_id=(me_outer, high * low_count + me_low), device_id_type=MESH
        )
    tell_group(barrier)
    for load in loads:
        load.wait()

    for mid in range(mids):
        lanes = slice(mid * LANES, (mid + 1) * LANES)
        block = panel_ref[:, lanes] * signs_ref[:, lanes].astype(jnp.float32)
        for peer in range(group):
            send1[peer, mid * SHARE:(mid + 1) * SHARE, :] = block[peer * SHARE:(peer + 1) * SHARE, :]

    pl.semaphore_wait(barrier, group - 1 + high_count - 1)

    copies = []
    for mask in sorted(range(1, group), key=lambda m: (bin(m).count("1"), m)):
        peer = flipped(me_group, mask, group)
        copy = pltpu.make_async_remote_copy(
            src_ref=send1.at[peer],
            dst_ref=recv1.at[me_group],
            send_sem=send1_sem.at[mask],
            recv_sem=recv1_sem.at[mask],
            device_id=(peer // low_count, me_high * low_count + peer % low_count),
            device_id_type=MESH,
        )
        copy.start()
        copies.append(copy)
    tell_group(ready_sem)
    recv1[me_group] = send1[me_group]

    span = 4 * LANES
    low_bits = log2(LANES)
    inner_bits = log2(inner_count)
    fold_bits = [log2(local_rows) + inner_bits + b for b in reversed(range(log2(outer_count)))]
    fold_bits += [log2(local_rows) + b for b in reversed(range(log2(low_count)))]
    fold_bits += [b for b in reversed(range(low_bits, log2(local_rows)))]

    def signs_of(chunk, carry):
        lanes = pl.ds(pl.multiple_of(chunk * span, span), span)
        kept = kept_ref[:, lanes]
        for place, bit in enumerate(fold_bits):
            bits_ref[place:place + 1, lanes] = sign_of_bit(kept, bit)
        plane = jnp.full((1, span), scale, jnp.float32)
        for bit in range(log2(high_count)):
            here = me_high // (1 << bit) % 2
            flip = sign_of_bit(kept, log2(local_rows * low_count) + bit)
            plane = plane * jnp.where(here == 1, flip, 1.0)
        bits_ref[len(fold_bits):len(fold_bits) + 1, lanes] = plane
        position = lax.broadcasted_iota(jnp.int32, (16, span), 0)
        base = jnp.ones((16, span), jnp.float32)
        for bit in range(4):
            taken = jnp.bitwise_and(jnp.right_shift(position, bit), 1) == 1
            base = base * jnp.where(taken, sign_of_bit(kept, bit), 1.0)
        for top in range(LANES // 16):
            block = base
            for bit in range(4, low_bits):
                if top >> (bit - 4) & 1:
                    block = block * sign_of_bit(kept, bit)
            block = block.astype(jnp.bfloat16)
            mix_ref[top * 16:(top + 1) * 16, lanes] = block
            mix_ref[LANES + top * 16:LANES + (top + 1) * 16, lanes] = block
        return carry

    lax.fori_loop(0, kept_count // span, signs_of, 0)

    for copy in copies:
        copy.wait_recv()

    gathered = recv1[...].reshape(group * rows, LANES)
    upper = gathered.astype(jnp.bfloat16)
    lower = (gathered - upper.astype(jnp.float32)).astype(jnp.bfloat16)
    both = jnp.concatenate([upper, lower], axis=1)

    pl.semaphore_wait(ready_sem, group - 1)
    mine = me_high * group + me_group
    width = low_count * LANES
    far = [(h, o) for h in reversed(range(high_count)) for o in reversed(range(outer_count))]
    sent = []
    for high_mask, outer_mask in far:
        high = flipped(me_high, high_mask, high_count)
        outer = flipped(me_outer, outer_mask, outer_count)
        block = outer * high_count + high
        lanes = pl.ds(pl.multiple_of(block * width, width), width)
        part = jnp.dot(both, mix_ref[:, lanes], preferred_element_type=jnp.float32)
        for place in range(len(fold_bits)):
            half = part.shape[0] // 2
            part = part[:half] + part[half:] * bits_ref[place:place + 1, lanes]
        part = part * bits_ref[len(fold_bits):len(fold_bits) + 1, lanes]
        for low in range(low_count):
            to = block * low_count + low
            send2[to] = part[:, low * LANES:(low + 1) * LANES]
            copy = pltpu.make_async_remote_copy(
                src_ref=send2.at[to],
                dst_ref=recv2.at[mine],
                send_sem=send2_sem.at[to],
                recv_sem=recv2_sem.at[mine],
                device_id=(outer, high * low_count + low),
                device_id_type=MESH,
            )
            if high_mask == 0 and outer_mask == 0:
                @pl.when(low != me_low)
                def _():
                    copy.start()
            else:
                copy.start()
    own = pltpu.make_async_copy(send2.at[me], recv2.at[mine], own_sem)
    own.start()

    def arrival(source):
        return pltpu.make_async_remote_copy(
            src_ref=send2.at[source],
            dst_ref=recv2.at[source],
            send_sem=send2_sem.at[source],
            recv_sem=recv2_sem.at[source],
            device_id=(me_outer, me_inner),
            device_id_type=MESH,
        )

    def await_arrival(step, carry):
        arrival((mine + step) % device_count).wait_recv()
        return carry

    lax.fori_loop(1, device_count, await_arrival, 0)

    def await_sent(step, carry):
        arrival((me + step) % device_count).wait_send()
        return carry

    lax.fori_loop(1, device_count, await_sent, 0)
    for copy in copies:
        copy.wait_send()
    own.wait()


def solution(mesh):
    outer_count, inner_count = mesh.shape["outer"], mesh.shape["inner"]
    device_count = outer_count * inner_count

    def local(matrix_panel, row_signs, kept_rows):
        columns, local_rows = matrix_panel.shape
        kept_count = kept_rows.shape[0]
        low_count = max(columns // (SHARE * outer_count), 1)
        fits = (
            low_count * outer_count * SHARE == columns
            and inner_count % low_count == 0
            and kept_count == device_count * LANES
            and local_rows % (2 * LANES) == 0
        )
        if not fits:
            return scatter_form(matrix_panel, row_signs, kept_rows)
        group = outer_count * low_count
        rows = local_rows // LANES * SHARE
        bits = log2(group) + log2(local_rows // LANES)
        arrived = pl.pallas_call(
            functools.partial(
                kernel, outer_count, inner_count, low_count, 1.0 / math.sqrt(local_rows * device_count)
            ),
            out_shape=jax.ShapeDtypeStruct((device_count, SHARE, LANES), jnp.float32),
            in_specs=[pl.BlockSpec(memory_space=pl.ANY)] * 3,
            out_specs=pl.BlockSpec(memory_space=pl.ANY),
            scratch_shapes=[
                pltpu.VMEM((columns, local_rows), jnp.float32),
                pltpu.VMEM((1, local_rows), jnp.int32),
                pltpu.VMEM((1, kept_count), jnp.int32),
                pltpu.SemaphoreType.DMA((3,)),
                pltpu.SemaphoreType.REGULAR,
                pltpu.VMEM((group, rows, LANES), jnp.float32),
                pltpu.VMEM((group, rows, LANES), jnp.float32),
                pltpu.VMEM((device_count, SHARE, LANES), jnp.float32),
                pltpu.VMEM((2 * LANES, kept_count), jnp.bfloat16),
                pltpu.VMEM((bits + 1, kept_count), jnp.float32),
                pltpu.SemaphoreType.DMA((group,)),
                pltpu.SemaphoreType.DMA((group,)),
                pltpu.SemaphoreType.DMA((device_count,)),
                pltpu.SemaphoreType.DMA((device_count,)),
                pltpu.SemaphoreType.DMA(()),
            ],
            compiler_params=pltpu.CompilerParams(collective_id=0, has_side_effects=True),
        )(matrix_panel, row_signs.reshape(1, local_rows), kept_rows.reshape(1, kept_count))
        planes = arrived.reshape(device_count // group, columns, LANES)
        return jnp.sum(planes, axis=0).T

    return jax.shard_map(
        local,
        mesh=mesh,
        in_specs=(P(None, ("outer", "inner")), P(("outer", "inner")), P()),
        out_specs=P(("outer", "inner"), None),
        check_vma=False,
    )
```

```python
import functools
import math

import jax
import jax.numpy as jnp
from jax import lax
from jax.experimental import pallas as pl
from jax.experimental.pallas import tpu as pltpu
from jax.sharding import PartitionSpec as P

MESH = pl.DeviceIdType.MESH
LANES = 128
SHARE = 4


def bit_parity(values):
    folded = jnp.bitwise_xor(values, jnp.right_shift(values, 16))
    folded = jnp.bitwise_xor(folded, jnp.right_shift(folded, 8))
    folded = jnp.bitwise_xor(folded, jnp.right_shift(folded, 4))
    folded = jnp.bitwise_xor(folded, jnp.right_shift(folded, 2))
    folded = jnp.bitwise_xor(folded, jnp.right_shift(folded, 1))
    return jnp.bitwise_and(folded, 1)


def hadamard(order_size):
    positions = lax.iota(jnp.int32, order_size)
    shared = jnp.bitwise_and(positions[:, None], positions[None, :])
    return jnp.where(bit_parity(shared) == 0, 1.0, -1.0).astype(jnp.float32)


def scatter_form(matrix_panel, row_signs, kept_rows):
    highest = lax.Precision.HIGHEST
    columns, local_rows = matrix_panel.shape
    outer_count = lax.axis_size("outer")
    inner_count = lax.axis_size("inner")
    device_count = outer_count * inner_count
    total_rows = local_rows * device_count
    me_outer = lax.axis_index("outer")
    me_inner = lax.axis_index("inner")
    signed = matrix_panel * row_signs.astype(jnp.float32)[None, :]
    leading = 128
    trailing = local_rows // leading
    blocks = signed.reshape(columns, leading, trailing)
    blocks = jnp.einsum("ap,jpq->jaq", hadamard(leading), blocks, precision=highest)
    blocks = jnp.einsum("bq,jaq->jab", hadamard(trailing), blocks, precision=highest)
    local_mix = blocks.reshape(columns, local_rows)
    low_bits = kept_rows % local_rows
    high_outer = kept_rows // (local_rows * inner_count)
    high_inner = kept_rows // local_rows % inner_count
    flips = bit_parity(jnp.bitwise_and(high_outer, me_outer)) + bit_parity(
        jnp.bitwise_and(high_inner, me_inner)
    )
    parity_sign = jnp.where(flips % 2 == 0, 1.0, -1.0).astype(jnp.float32)
    values = jnp.take(local_mix, low_bits, axis=1)
    summed = lax.psum_scatter(
        (values * parity_sign[None, :]).T, ("outer", "inner"), scatter_dimension=0, tiled=True
    )
    return summed * (1.0 / math.sqrt(total_rows))


def flipped(index, mask, size):
    result, bit = 0, 1
    while bit < size:
        digit = index // bit % 2
        result = result + (1 - digit if mask & bit else digit) * bit
        bit *= 2
    return result


def log2(size):
    return size.bit_length() - 1


def sign_of_bit(rows, bit):
    return (1 - 2 * jnp.bitwise_and(jnp.right_shift(rows, bit), 1)).astype(jnp.float32)


def kernel(
    outer_count, inner_count, low_count, scale,
    panel_hbm, signs_hbm, kept_hbm, recv2,
    panel_ref, signs_ref, kept_ref, load_sem, ready_sem,
    send1, recv1, send2, mix_ref, bits_ref,
    send1_sem, recv1_sem, send2_sem, recv2_sem, own_sem,
):
    device_count = outer_count * inner_count
    high_count = inner_count // low_count
    group = outer_count * low_count
    columns, local_rows = panel_hbm.shape
    kept_count = kept_hbm.shape[1]
    mids = local_rows // LANES
    rows = mids * SHARE
    me_outer = lax.axis_index("outer")
    me_inner = lax.axis_index("inner")
    me = me_outer * inner_count + me_inner
    me_high = me_inner // low_count
    me_low = me_inner % low_count
    me_group = me_outer * low_count + me_low

    barrier = pltpu.get_barrier_semaphore()

    loads = [
        pltpu.make_async_copy(source, target, load_sem.at[place])
        for place, (source, target) in enumerate(
            [(panel_hbm, panel_ref), (signs_hbm, signs_ref), (kept_hbm, kept_ref)]
        )
    ]
    for load in loads:
        load.start()

    def tell_group(semaphore):
        for step in range(1, group):
            peer = (me_group + step) % group
            pl.semaphore_signal(
                semaphore,
                inc=1,
                device_id=(peer // low_count, me_high * low_count + peer % low_count),
                device_id_type=MESH,
            )

    for step in range(1, high_count):
        high = (me_high + step) % high_count
        pl.semaphore_signal(
            barrier, inc=1, device_id=(me_outer, high * low_count + me_low), device_id_type=MESH
        )
    tell_group(barrier)
    for load in loads:
        load.wait()

    for mid in range(mids):
        lanes = slice(mid * LANES, (mid + 1) * LANES)
        block = panel_ref[:, lanes] * signs_ref[:, lanes].astype(jnp.float32)
        for peer in range(group):
            send1[peer, mid * SHARE:(mid + 1) * SHARE, :] = block[peer * SHARE:(peer + 1) * SHARE, :]

    pl.semaphore_wait(barrier, group - 1 + high_count - 1)

    copies = []
    for mask in sorted(range(1, group), key=lambda m: (bin(m).count("1"), m)):
        peer = flipped(me_group, mask, group)
        copy = pltpu.make_async_remote_copy(
            src_ref=send1.at[peer],
            dst_ref=recv1.at[me_group],
            send_sem=send1_sem.at[mask],
            recv_sem=recv1_sem.at[mask],
            device_id=(peer // low_count, me_high * low_count + peer % low_count),
            device_id_type=MESH,
        )
        copy.start()
        copies.append(copy)
    tell_group(ready_sem)
    recv1[me_group] = send1[me_group]

    span = 4 * LANES
    low_bits = log2(LANES)
    inner_bits = log2(inner_count)
    fold_bits = [log2(local_rows) + inner_bits + b for b in reversed(range(log2(outer_count)))]
    fold_bits += [log2(local_rows) + b for b in reversed(range(log2(low_count)))]
    fold_bits += [b for b in reversed(range(low_bits, log2(local_rows)))]

    def signs_of(chunk, carry):
        lanes = pl.ds(pl.multiple_of(chunk * span, span), span)
        kept = kept_ref[:, lanes]
        for place, bit in enumerate(fold_bits):
            bits_ref[place:place + 1, lanes] = sign_of_bit(kept, bit)
        plane = jnp.full((1, span), scale, jnp.float32)
        for bit in range(log2(high_count)):
            here = me_high // (1 << bit) % 2
            flip = sign_of_bit(kept, log2(local_rows * low_count) + bit)
            plane = plane * jnp.where(here == 1, flip, 1.0)
        bits_ref[len(fold_bits):len(fold_bits) + 1, lanes] = plane
        position = lax.broadcasted_iota(jnp.int32, (16, span), 0)
        base = jnp.ones((16, span), jnp.float32)
        for bit in range(4):
            taken = jnp.bitwise_and(jnp.right_shift(position, bit), 1) == 1
            base = base * jnp.where(taken, sign_of_bit(kept, bit), 1.0)
        for top in range(LANES // 16):
            block = base
            for bit in range(4, low_bits):
                if top >> (bit - 4) & 1:
                    block = block * sign_of_bit(kept, bit)
            block = block.astype(jnp.bfloat16)
            mix_ref[top * 16:(top + 1) * 16, lanes] = block
            mix_ref[LANES + top * 16:LANES + (top + 1) * 16, lanes] = block
        return carry

    lax.fori_loop(0, kept_count // span, signs_of, 0)

    for copy in copies:
        copy.wait_recv()

    gathered = recv1[...].reshape(group * rows, LANES)
    upper = gathered.astype(jnp.bfloat16)
    lower = (gathered - upper.astype(jnp.float32)).astype(jnp.bfloat16)
    both = jnp.concatenate([upper, lower], axis=1)

    pl.semaphore_wait(ready_sem, group - 1)
    mine = me_high * group + me_group
    width = low_count * LANES
    far = [(h, o) for h in reversed(range(high_count)) for o in reversed(range(outer_count))]
    together = 2
    for first in range(0, len(far), together):
        places = []
        for high_mask, outer_mask in far[first:first + together]:
            high = flipped(me_high, high_mask, high_count)
            outer = flipped(me_outer, outer_mask, outer_count)
            block = outer * high_count + high
            lanes = pl.ds(pl.multiple_of(block * width, width), width)
            places.append((high_mask == 0 and outer_mask == 0, high, outer, block, lanes))
        parts = [
            jnp.dot(both, mix_ref[:, place[4]], preferred_element_type=jnp.float32) for place in places
        ]
        signs = [
            [jnp.broadcast_to(bits_ref[bit:bit + 1, place[4]], (2 * SHARE, width)) for bit in range(len(fold_bits) + 1)]
            for place in places
        ]

        def fold(start, size, bit):
            if size == 2 * SHARE:
                return [part[start:start + size] for part in parts]
            half = size // 2
            left, right = fold(start, half, bit + 1), fold(start + half, half, bit + 1)
            return [a + b * sign[bit] for a, b, sign in zip(left, right, signs)]

        for (last, high, outer, block, lanes), tile, sign in zip(places, fold(0, group * rows, 0), signs):
            bit = len(fold_bits) - 1
            part = (tile[:SHARE] + tile[SHARE:] * sign[bit][:SHARE]) * sign[bit + 1][:SHARE]
            for low in range(low_count):
                to = block * low_count + low
                send2[to] = part[:, low * LANES:(low + 1) * LANES]
                copy = pltpu.make_async_remote_copy(
                    src_ref=send2.at[to],
                    dst_ref=recv2.at[mine],
                    send_sem=send2_sem.at[to],
                    recv_sem=recv2_sem.at[mine],
                    device_id=(outer, high * low_count + low),
                    device_id_type=MESH,
                )
                if last:
                    @pl.when(low != me_low)
                    def _(copy=copy):
                        copy.start()
                else:
                    copy.start()
    own = pltpu.make_async_copy(send2.at[me], recv2.at[mine], own_sem)
    own.start()

    def arrival(source):
        return pltpu.make_async_remote_copy(
            src_ref=send2.at[source],
            dst_ref=recv2.at[source],
            send_sem=send2_sem.at[source],
            recv_sem=recv2_sem.at[source],
            device_id=(me_outer, me_inner),
            device_id_type=MESH,
        )

    def await_arrival(step, carry):
        arrival((mine + step) % device_count).wait_recv()
        return carry

    lax.fori_loop(1, device_count, await_arrival, 0)

    def await_sent(step, carry):
        arrival((me + step) % device_count).wait_send()
        return carry

    lax.fori_loop(1, device_count, await_sent, 0)
    for copy in copies:
        copy.wait_send()
    own.wait()


def solution(mesh):
    outer_count, inner_count = mesh.shape["outer"], mesh.shape["inner"]
    device_count = outer_count * inner_count

    def local(matrix_panel, row_signs, kept_rows):
        columns, local_rows = matrix_panel.shape
        kept_count = kept_rows.shape[0]
        low_count = max(columns // (SHARE * outer_count), 1)
        fits = (
            low_count * outer_count * SHARE == columns
            and inner_count % low_count == 0
            and kept_count == device_count * LANES
            and local_rows % (2 * LANES) == 0
        )
        if not fits:
            return scatter_form(matrix_panel, row_signs, kept_rows)
        group = outer_count * low_count
        rows = local_rows // LANES * SHARE
        bits = log2(group) + log2(local_rows // LANES)
        arrived = pl.pallas_call(
            functools.partial(
                kernel, outer_count, inner_count, low_count, 1.0 / math.sqrt(local_rows * device_count)
            ),
            out_shape=jax.ShapeDtypeStruct((device_count, SHARE, LANES), jnp.float32),
            in_specs=[pl.BlockSpec(memory_space=pl.ANY)] * 3,
            out_specs=pl.BlockSpec(memory_space=pl.ANY),
            scratch_shapes=[
                pltpu.VMEM((columns, local_rows), jnp.float32),
                pltpu.VMEM((1, local_rows), jnp.int32),
                pltpu.VMEM((1, kept_count), jnp.int32),
                pltpu.SemaphoreType.DMA((3,)),
                pltpu.SemaphoreType.REGULAR,
                pltpu.VMEM((group, rows, LANES), jnp.float32),
                pltpu.VMEM((group, rows, LANES), jnp.float32),
                pltpu.VMEM((device_count, SHARE, LANES), jnp.float32),
                pltpu.VMEM((2 * LANES, kept_count), jnp.bfloat16),
                pltpu.VMEM((bits + 1, kept_count), jnp.float32),
                pltpu.SemaphoreType.DMA((group,)),
                pltpu.SemaphoreType.DMA((group,)),
                pltpu.SemaphoreType.DMA((device_count,)),
                pltpu.SemaphoreType.DMA((device_count,)),
                pltpu.SemaphoreType.DMA(()),
            ],
            compiler_params=pltpu.CompilerParams(collective_id=0, has_side_effects=True),
        )(matrix_panel, row_signs.reshape(1, local_rows), kept_rows.reshape(1, kept_count))
        planes = arrived.reshape(device_count // group, columns, LANES)
        return jnp.sum(planes, axis=0).T

    return jax.shard_map(
        local,
        mesh=mesh,
        in_specs=(P(None, ("outer", "inner")), P(("outer", "inner")), P()),
        out_specs=P(("outer", "inner"), None),
        check_vma=False,
    )
```

```python
import functools
import math

import jax
import jax.numpy as jnp
from jax import lax
from jax.experimental import pallas as pl
from jax.experimental.pallas import tpu as pltpu
from jax.sharding import PartitionSpec as P

MESH = pl.DeviceIdType.MESH
LANES = 128
SHARE = 4


def bit_parity(values):
    folded = jnp.bitwise_xor(values, jnp.right_shift(values, 16))
    folded = jnp.bitwise_xor(folded, jnp.right_shift(folded, 8))
    folded = jnp.bitwise_xor(folded, jnp.right_shift(folded, 4))
    folded = jnp.bitwise_xor(folded, jnp.right_shift(folded, 2))
    folded = jnp.bitwise_xor(folded, jnp.right_shift(folded, 1))
    return jnp.bitwise_and(folded, 1)


def hadamard(order_size):
    positions = lax.iota(jnp.int32, order_size)
    shared = jnp.bitwise_and(positions[:, None], positions[None, :])
    return jnp.where(bit_parity(shared) == 0, 1.0, -1.0).astype(jnp.float32)


def scatter_form(matrix_panel, row_signs, kept_rows):
    highest = lax.Precision.HIGHEST
    columns, local_rows = matrix_panel.shape
    outer_count = lax.axis_size("outer")
    inner_count = lax.axis_size("inner")
    device_count = outer_count * inner_count
    total_rows = local_rows * device_count
    me_outer = lax.axis_index("outer")
    me_inner = lax.axis_index("inner")
    signed = matrix_panel * row_signs.astype(jnp.float32)[None, :]
    leading = 128
    trailing = local_rows // leading
    blocks = signed.reshape(columns, leading, trailing)
    blocks = jnp.einsum("ap,jpq->jaq", hadamard(leading), blocks, precision=highest)
    blocks = jnp.einsum("bq,jaq->jab", hadamard(trailing), blocks, precision=highest)
    local_mix = blocks.reshape(columns, local_rows)
    low_bits = kept_rows % local_rows
    high_outer = kept_rows // (local_rows * inner_count)
    high_inner = kept_rows // local_rows % inner_count
    flips = bit_parity(jnp.bitwise_and(high_outer, me_outer)) + bit_parity(
        jnp.bitwise_and(high_inner, me_inner)
    )
    parity_sign = jnp.where(flips % 2 == 0, 1.0, -1.0).astype(jnp.float32)
    values = jnp.take(local_mix, low_bits, axis=1)
    summed = lax.psum_scatter(
        (values * parity_sign[None, :]).T, ("outer", "inner"), scatter_dimension=0, tiled=True
    )
    return summed * (1.0 / math.sqrt(total_rows))


def flipped(index, mask, size):
    result, bit = 0, 1
    while bit < size:
        digit = index // bit % 2
        result = result + (1 - digit if mask & bit else digit) * bit
        bit *= 2
    return result


def log2(size):
    return size.bit_length() - 1


def sign_of_bit(rows, bit):
    return (1 - 2 * jnp.bitwise_and(jnp.right_shift(rows, bit), 1)).astype(jnp.float32)


def kernel(
    outer_count, inner_count, low_count, scale,
    panel_hbm, signs_hbm, kept_hbm, recv2,
    panel_ref, signs_ref, kept_ref, load_sem, ready_sem, line_sem,
    send1, recv1, send2, mix_ref, bits_ref,
    send1_sem, recv1_sem, send2_sem, recv2_sem, own_sem,
):
    device_count = outer_count * inner_count
    high_count = inner_count // low_count
    group = outer_count * low_count
    columns, local_rows = panel_hbm.shape
    kept_count = kept_hbm.shape[1]
    mids = local_rows // LANES
    rows = mids * SHARE
    me_outer = lax.axis_index("outer")
    me_inner = lax.axis_index("inner")
    me = me_outer * inner_count + me_inner
    me_high = me_inner // low_count
    me_low = me_inner % low_count
    me_group = me_outer * low_count + me_low

    barrier = pltpu.get_barrier_semaphore()

    loads = [
        pltpu.make_async_copy(source, target, load_sem.at[place])
        for place, (source, target) in enumerate(
            [(panel_hbm, panel_ref), (signs_hbm, signs_ref), (kept_hbm, kept_ref)]
        )
    ]
    for load in loads:
        load.start()

    def tell_group(semaphore):
        for step in range(1, group):
            peer = (me_group + step) % group
            pl.semaphore_signal(
                semaphore,
                inc=1,
                device_id=(peer // low_count, me_high * low_count + peer % low_count),
                device_id_type=MESH,
            )

    def tell_line(semaphore):
        for step in (-1, 1):
            high = me_high + step

            @pl.when((high >= 0) & (high < high_count))
            def _(high=high):
                pl.semaphore_signal(
                    semaphore, inc=1, device_id=(me_outer, high * low_count + me_low), device_id_type=MESH
                )

    line = jnp.where(me_high > 0, 1, 0) + jnp.where(me_high < high_count - 1, 1, 0)
    tell_line(barrier)
    tell_group(barrier)
    for load in loads:
        load.wait()

    for mid in range(mids):
        lanes = slice(mid * LANES, (mid + 1) * LANES)
        block = panel_ref[:, lanes] * signs_ref[:, lanes].astype(jnp.float32)
        for peer in range(group):
            send1[peer, mid * SHARE:(mid + 1) * SHARE, :] = block[peer * SHARE:(peer + 1) * SHARE, :]

    pl.semaphore_wait(barrier, group - 1 + line)

    copies = []
    for mask in sorted(range(1, group), key=lambda m: (bin(m).count("1"), m)):
        peer = flipped(me_group, mask, group)
        copy = pltpu.make_async_remote_copy(
            src_ref=send1.at[peer],
            dst_ref=recv1.at[me_group],
            send_sem=send1_sem.at[mask],
            recv_sem=recv1_sem.at[mask],
            device_id=(peer // low_count, me_high * low_count + peer % low_count),
            device_id_type=MESH,
        )
        copy.start()
        copies.append(copy)
    recv1[me_group] = send1[me_group]

    span = 4 * LANES
    low_bits = log2(LANES)
    inner_bits = log2(inner_count)
    fold_bits = [log2(local_rows) + inner_bits + b for b in reversed(range(log2(outer_count)))]
    fold_bits += [log2(local_rows) + b for b in reversed(range(log2(low_count)))]
    fold_bits += [b for b in reversed(range(low_bits, log2(local_rows)))]

    def signs_of(chunk, carry):
        lanes = pl.ds(pl.multiple_of(chunk * span, span), span)
        kept = kept_ref[:, lanes]
        for place, bit in enumerate(fold_bits):
            bits_ref[place:place + 1, lanes] = sign_of_bit(kept, bit)
        plane = jnp.full((1, span), scale, jnp.float32)
        for bit in range(log2(high_count)):
            here = me_high // (1 << bit) % 2
            flip = sign_of_bit(kept, log2(local_rows * low_count) + bit)
            plane = plane * jnp.where(here == 1, flip, 1.0)
        bits_ref[len(fold_bits):len(fold_bits) + 1, lanes] = plane
        position = lax.broadcasted_iota(jnp.int32, (16, span), 0)
        base = jnp.ones((16, span), jnp.float32)
        for bit in range(4):
            taken = jnp.bitwise_and(jnp.right_shift(position, bit), 1) == 1
            base = base * jnp.where(taken, sign_of_bit(kept, bit), 1.0)
        for top in range(LANES // 16):
            block = base
            for bit in range(4, low_bits):
                if top >> (bit - 4) & 1:
                    block = block * sign_of_bit(kept, bit)
            block = block.astype(jnp.bfloat16)
            mix_ref[top * 16:(top + 1) * 16, lanes] = block
            mix_ref[LANES + top * 16:LANES + (top + 1) * 16, lanes] = block
        return carry

    rounds = max(high_count - 2, 0)
    spans = kept_count // span
    for turn in range(rounds):
        tell_line(line_sem.at[turn])
        lax.fori_loop(spans * turn // rounds, spans * (turn + 1) // rounds, signs_of, 0)
        pl.semaphore_wait(line_sem.at[turn], line)
    if not rounds:
        lax.fori_loop(0, spans, signs_of, 0)
    tell_group(ready_sem)

    for copy in copies:
        copy.wait_recv()

    gathered = recv1[...].reshape(group * rows, LANES)
    upper = gathered.astype(jnp.bfloat16)
    lower = (gathered - upper.astype(jnp.float32)).astype(jnp.bfloat16)
    both = jnp.concatenate([upper, lower], axis=1)

    pl.semaphore_wait(ready_sem, group - 1)
    mine = me_high * group + me_group
    width = low_count * LANES
    far = [(h, o) for h in reversed(range(high_count)) for o in reversed(range(outer_count))]
    together = 2
    for first in range(0, len(far), together):
        places = []
        for high_mask, outer_mask in far[first:first + together]:
            high = flipped(me_high, high_mask, high_count)
            outer = flipped(me_outer, outer_mask, outer_count)
            block = outer * high_count + high
            lanes = pl.ds(pl.multiple_of(block * width, width), width)
            places.append((high_mask == 0 and outer_mask == 0, high, outer, block, lanes))
        parts = [
            jnp.dot(both, mix_ref[:, place[4]], preferred_element_type=jnp.float32) for place in places
        ]
        signs = [
            [jnp.broadcast_to(bits_ref[bit:bit + 1, place[4]], (2 * SHARE, width)) for bit in range(len(fold_bits) + 1)]
            for place in places
        ]

        def fold(start, size, bit):
            if size == 2 * SHARE:
                return [part[start:start + size] for part in parts]
            half = size // 2
            left, right = fold(start, half, bit + 1), fold(start + half, half, bit + 1)
            return [a + b * sign[bit] for a, b, sign in zip(left, right, signs)]

        for (last, high, outer, block, lanes), tile, sign in zip(places, fold(0, group * rows, 0), signs):
            bit = len(fold_bits) - 1
            part = (tile[:SHARE] + tile[SHARE:] * sign[bit][:SHARE]) * sign[bit + 1][:SHARE]
            for low in range(low_count):
                to = block * low_count + low
                send2[to] = part[:, low * LANES:(low + 1) * LANES]
                copy = pltpu.make_async_remote_copy(
                    src_ref=send2.at[to],
                    dst_ref=recv2.at[mine],
                    send_sem=send2_sem.at[to],
                    recv_sem=recv2_sem.at[mine],
                    device_id=(outer, high * low_count + low),
                    device_id_type=MESH,
                )
                if last:
                    @pl.when(low != me_low)
                    def _(copy=copy):
                        copy.start()
                else:
                    copy.start()
    own = pltpu.make_async_copy(send2.at[me], recv2.at[mine], own_sem)
    own.start()

    def arrival(source):
        return pltpu.make_async_remote_copy(
            src_ref=send2.at[source],
            dst_ref=recv2.at[source],
            send_sem=send2_sem.at[source],
            recv_sem=recv2_sem.at[source],
            device_id=(me_outer, me_inner),
            device_id_type=MESH,
        )

    def await_arrival(step, carry):
        arrival((mine + step) % device_count).wait_recv()
        return carry

    lax.fori_loop(1, device_count, await_arrival, 0)

    def await_sent(step, carry):
        arrival((me + step) % device_count).wait_send()
        return carry

    lax.fori_loop(1, device_count, await_sent, 0)
    for copy in copies:
        copy.wait_send()
    own.wait()


def solution(mesh):
    outer_count, inner_count = mesh.shape["outer"], mesh.shape["inner"]
    device_count = outer_count * inner_count

    def local(matrix_panel, row_signs, kept_rows):
        columns, local_rows = matrix_panel.shape
        kept_count = kept_rows.shape[0]
        low_count = max(columns // (SHARE * outer_count), 1)
        fits = (
            low_count * outer_count * SHARE == columns
            and inner_count % low_count == 0
            and kept_count == device_count * LANES
            and local_rows % (2 * LANES) == 0
        )
        if not fits:
            return scatter_form(matrix_panel, row_signs, kept_rows)
        group = outer_count * low_count
        rows = local_rows // LANES * SHARE
        bits = log2(group) + log2(local_rows // LANES)
        arrived = pl.pallas_call(
            functools.partial(
                kernel, outer_count, inner_count, low_count, 1.0 / math.sqrt(local_rows * device_count)
            ),
            out_shape=jax.ShapeDtypeStruct((device_count, SHARE, LANES), jnp.float32),
            in_specs=[pl.BlockSpec(memory_space=pl.ANY)] * 3,
            out_specs=pl.BlockSpec(memory_space=pl.ANY),
            scratch_shapes=[
                pltpu.VMEM((columns, local_rows), jnp.float32),
                pltpu.VMEM((1, local_rows), jnp.int32),
                pltpu.VMEM((1, kept_count), jnp.int32),
                pltpu.SemaphoreType.DMA((3,)),
                pltpu.SemaphoreType.REGULAR,
                pltpu.SemaphoreType.REGULAR((max(inner_count // low_count - 2, 1),)),
                pltpu.VMEM((group, rows, LANES), jnp.float32),
                pltpu.VMEM((group, rows, LANES), jnp.float32),
                pltpu.VMEM((device_count, SHARE, LANES), jnp.float32),
                pltpu.VMEM((2 * LANES, kept_count), jnp.bfloat16),
                pltpu.VMEM((bits + 1, kept_count), jnp.float32),
                pltpu.SemaphoreType.DMA((group,)),
                pltpu.SemaphoreType.DMA((group,)),
                pltpu.SemaphoreType.DMA((device_count,)),
                pltpu.SemaphoreType.DMA((device_count,)),
                pltpu.SemaphoreType.DMA(()),
            ],
            compiler_params=pltpu.CompilerParams(collective_id=0, has_side_effects=True),
        )(matrix_panel, row_signs.reshape(1, local_rows), kept_rows.reshape(1, kept_count))
        planes = arrived.reshape(device_count // group, columns, LANES)
        return jnp.sum(planes, axis=0).T

    return jax.shard_map(
        local,
        mesh=mesh,
        in_specs=(P(None, ("outer", "inner")), P(("outer", "inner")), P()),
        out_specs=P(("outer", "inner"), None),
        check_vma=False,
    )
```
